32 devices in a mesh: dp: 16 (over z, y, x), tensor: 2 (over core).
Axes of the slice: x: 2, y: 2, z: 4, core: 2. Of those that a mesh axis runs over, the one named last changes fastest.
Arguments:
- tokens: bfloat16 [2048, 1024], P('dp'), may hold values from -6 to 6
- segment_ids: int32 [2048], P('dp'), may hold values from 0 to 7, never falling along the last dimension, each value on 1 to 512 neighbouring positions
- attn_gain: bfloat16 [1024], P('dp'), may hold values from 0.5 to 1.5
- query_weight: bfloat16 [1024, 512], P('dp', 'tensor'), may hold values from -0.1875 to 0.1875
- key_weight: bfloat16 [1024, 512], P('dp', 'tensor'), may hold values from -0.1875 to 0.1875
- value_weight: bfloat16 [1024, 1024], P('dp', 'tensor'), may hold values from -0.1875 to 0.1875
- gate_weight: bfloat16 [1024, 1024], P('dp', 'tensor'), may hold values from -0.1875 to 0.1875
- low_weight: bfloat16 [1024, 16], P('dp'), may hold values from -0.1875 to 0.1875
- rise_weight: bfloat16 [4, 16, 128], P('tensor', None, 'dp'), may hold values from -1.5 to 1.5
- decay_bias: bfloat16 [4, 128], P('tensor', 'dp'), may hold values from -2 to 11
- head_gain: bfloat16 [256], P('dp'), may hold values from 0.5 to 1.5
- out_weight: bfloat16 [1024, 1024], P('dp', 'tensor'), may hold values from -0.1875 to 0.1875
- ffn_gain: bfloat16 [1024], P('dp'), may hold values from 0.5 to 1.5
- ffn_gate: bfloat16 [1024, 2816], P('dp', 'tensor'), may hold values from -0.1875 to 0.1875
- ffn_up: bfloat16 [1024, 2816], P('dp', 'tensor'), may hold values from -0.1875 to 0.1875
- ffn_down: bfloat16 [1024, 2816], P('dp', 'tensor'), may hold values from -0.109375 to 0.109375
- cotangent: bfloat16 [2048, 1024], P('dp'), may hold values from -6 to 6
Outputs:
- output: bfloat16 [2048, 1024], P('dp')
- tokens_grad: float32 [2048, 1024], P('dp')
- attn_gain_grad: float32 [1024], P('dp')
- query_grad: float32 [1024, 512], P('dp', 'tensor')
- key_grad: float32 [1024, 512], P('dp', 'tensor')
- value_grad: float32 [1024, 1024], P('dp', 'tensor')
- gate_grad: float32 [1024, 1024], P('dp', 'tensor')
- low_grad: float32 [1024, 16], P('dp')
- rise_grad: float32 [4, 16, 128], P('tensor', None, 'dp')
- bias_grad: float32 [4, 128], P('tensor', 'dp')
- head_gain_grad: float32 [256], P('dp')
- out_grad: float32 [1024, 1024], P('dp', 'tensor')
- ffn_gain_grad: float32 [1024], P('dp')
- ffn_gate_grad: float32 [1024, 2816], P('dp', 'tensor')
- ffn_up_grad: float32 [1024, 2816], P('dp', 'tensor')
- ffn_down_grad: float32 [1024, 2816], P('dp', 'tensor')
The draws below stay inside these ranges and needn't reach their ends.
Inputs may be any that keep to these rules, and one draw needn't show every extreme that they name: `segment_ids`: segment numbers never fall along the tokens; each of the 8 segments holds 1 to 512 consecutive tokens and one holds exactly 512.
All inputs are finite; a program needn't handle non-finite values.
Results may differ from the reference program's by a relative error of at most 0.039.
Values may be sent and summed in bfloat16 or wider, within the bound.
A program may use at most 128 MiB of HBM per device.

```python
import math
import jax
import jax.numpy as jnp
import numpy as np
from jax import lax

D = 1024
H = 4
DK = 128
DV = 256
R = 16
FF = 2816
TOKENS = 2048
SEQ = 512
SEGS = 8


def raised(values, own_key, source, target, parts, factor):
    def block_of(axis_at):
        return (jnp.arange(values.shape[axis_at]) // (values.shape[axis_at] // parts)).reshape((-1,) + (1,) * (values.ndim - 1 - axis_at))

    one_side = jax.random.permutation(own_key, parts)[block_of(target)]
    far = (block_of(target) + parts // 2) % parts
    return jnp.where((block_of(source) == one_side) | (block_of(source) == far), factor * values, values)


def levels(stream_key, shape, cuts, least, top_value):
    factor_of, own = 1.0, jax.random.fold_in(stream_key, 6)
    for dim, shards_of in cuts:
        draws = jnp.exp(jax.random.uniform(jax.random.fold_in(own, dim), (shards_of,), jnp.float32, least / len(cuts), top_value / len(cuts)))
        factor_of = factor_of * jnp.repeat(draws, shape[dim] // shards_of).reshape([-1 if axis == dim else 1 for axis in range(len(shape))])
    return factor_of


def split_up(amount, total, most, skew):
    loads = [(1 << 20) // math.isqrt(rank ** skew) + 1 for rank in range(2, amount + 1)]
    rest, given = total - most - (amount - 1), [1] * (amount - 1)
    while rest > 0:
        movable = [i for i in range(amount - 1) if given[i] < most]
        whole, budget = sum([loads[i] for i in movable]), rest
        for i in movable:
            extra = min(most - given[i], max(1, budget * loads[i] // whole), rest)
            given[i] = given[i] + extra
            rest = rest - extra
    return np.array([most] + given)


def ragged_sizes(rng, count, total, bound, skew):
    if count == 2:
        one = jax.random.randint(rng, (), max(1, total - bound), min(bound, total - 1) + 1)
        return jnp.stack([one, total - one])
    tallies = jnp.asarray(split_up(count, total, bound, skew), jnp.int32)
    pairs = (count - 1) // 2
    giver, sink = tallies[1:1 + 2 * pairs:2], tallies[2:2 + 2 * pairs:2]
    slack = jnp.minimum(giver - 1, bound - sink)
    moved = jax.random.randint(jax.random.fold_in(rng, 1), (pairs,), 0, 1 << 20) % (slack + 1)
    tallies = tallies.at[1:1 + 2 * pairs:2].set(giver - moved).at[2:2 + 2 * pairs:2].set(sink + moved)
    return tallies[jax.random.permutation(jax.random.fold_in(rng, 2), count)]


def noise(rng, shape, scale, limit, shards=(), dtype=jnp.bfloat16):
    factor_of = levels(rng, shape, shards, -0.22, 0.18) if shards else 1.0
    result = jax.random.normal(rng, shape, jnp.float32) * scale * factor_of
    return jnp.minimum(jnp.maximum(result, -limit), limit).astype(dtype)


def heavy_noise(rng, dims, scale, most, cuts, heavy, held_as=jnp.bfloat16):
    values = scale * jax.random.normal(rng, dims, jnp.float32)
    if cuts:
        values = values * levels(rng, dims, cuts, -0.22, 0.18)
    return jnp.clip(raised(values, jax.random.fold_in(rng, 3), *heavy), -most, most).astype(held_as)


def setup_inputs(seed: int = 0) -> dict:
    keys = jax.random.split(jax.random.key(seed), 18)
    return {
        "tokens": heavy_noise(keys[0], (TOKENS, D), 1.0, 6.0, ((0, 16),), (0, 1, 16, 2.0)),
        "segment_ids": jnp.searchsorted(jnp.cumsum(ragged_sizes(keys[1], SEGS, TOKENS, SEQ, 1)), jnp.arange(TOKENS), side="right").astype(jnp.int32),
        "attn_gain": jnp.clip(1.0 + 0.1 * jax.random.normal(keys[2], (D,), jnp.float32), 0.5, 1.5).astype(jnp.bfloat16),
        "query_weight": noise(keys[3], (D, H * DK), D ** -0.5, 0.1875, ((0, 16), (1, 2))),
        "key_weight": noise(keys[4], (D, H * DK), D ** -0.5, 0.1875, ((0, 16), (1, 2))),
        "value_weight": noise(keys[5], (D, H * DV), D ** -0.5, 0.1875, ((0, 16), (1, 2))),
        "gate_weight": noise(keys[6], (D, H * DV), D ** -0.5, 0.1875, ((0, 16), (1, 2))),
        "low_weight": noise(keys[7], (D, R), D ** -0.5, 0.1875, ((0, 16),)),
        "rise_weight": noise(keys[8], (H, R, DK), R ** -0.5, 1.5, ((0, 2), (2, 16))),
        "decay_bias": jnp.clip(-2.0 + 13.0 * jax.random.uniform(keys[9], (H, DK), jnp.float32) ** levels(keys[9], (H, DK), ((0, 2), (1, 16)), -0.2, 0.2), -2.0, 11.0).astype(jnp.bfloat16),
        "head_gain": jnp.clip(1.0 + 0.1 * jax.random.normal(keys[10], (DV,), jnp.float32), 0.5, 1.5).astype(jnp.bfloat16),
        "out_weight": noise(keys[11], (D, H * DV), (H * DV) ** -0.5, 0.1875, ((0, 16), (1, 2))),
        "ffn_gain": jnp.clip(1.0 + 0.1 * jax.random.normal(keys[12], (D,), jnp.float32), 0.5, 1.5).astype(jnp.bfloat16),
        "ffn_gate": noise(keys[13], (D, FF), D ** -0.5, 0.1875, ((0, 16), (1, 2))),
        "ffn_up": noise(keys[14], (D, FF), D ** -0.5, 0.1875, ((0, 16), (1, 2))),
        "ffn_down": noise(keys[15], (D, FF), FF ** -0.5, 0.109375, ((0, 16), (1, 2))),
        "cotangent": heavy_noise(keys[16], (TOKENS, D), 1.0, 6.0, ((0, 16),), (0, 1, 16, 2.0)),
    }


epsilon = 1e-06
head_epsilon = 1.0
gate_scale = 16.0
highest = lax.Precision.HIGHEST

def matmul(left, right):
    return jnp.dot(left, right, preferred_element_type=jnp.float32)

def matmul_nt(left, right):
    return lax.dot_general(left, right, (((1,), (1,)), ((), ())), preferred_element_type=jnp.float32)

def matmul_tn(left, right):
    return lax.dot_general(left, right, (((0,), (0,)), ((), ())), preferred_element_type=jnp.float32)

def inverse_rms(entries, small=epsilon):
    return lax.rsqrt(lax.optimization_barrier(jnp.mean(entries * entries, axis=-1, keepdims=True)) + small)

def norm_back(entries, inverse, scale_by, grad):
    scaled = grad * scale_by
    return inverse * scaled - entries * inverse ** 3 * lax.optimization_barrier(jnp.mean(scaled * entries, axis=-1, keepdims=True))

def silu_parts(pre_act):
    logistic = jax.nn.sigmoid(pre_act)
    return (pre_act * logistic, logistic * (1.0 + pre_act * (1.0 - logistic)))

def pair_decay(cumul, seg_ids):
    places = jnp.arange(seg_ids.shape[0])
    allowed = ((places[:, None] >= places[None, :]) & (seg_ids[:, None] == seg_ids[None, :])).astype(jnp.float32)
    spread = jnp.minimum(cumul[:, None] - cumul[None, :], 0.0)
    return (jnp.exp(spread) * allowed[:, :, None, None], allowed)

def block_forward(states, seg_before, queries, key_rows, values, decays, seg_ids):
    cumul = jnp.cumsum(decays, axis=0)
    pairs, allowed = pair_decay(cumul, seg_ids)
    carry = (seg_ids == seg_before).astype(jnp.float32)
    scores = jnp.einsum('thd,shd,tshd->hts', queries, key_rows, pairs, precision=highest)
    mixed = jnp.einsum('hts,shv->thv', scores, values, precision=highest)
    rising = jnp.exp(cumul) * carry[:, None, None]
    mixed = mixed + jnp.einsum('thd,hdv->thv', queries * rising, states, precision=highest)
    final = cumul[-1]
    tail = jnp.exp(final[None] - cumul) * (seg_ids == seg_ids[-1]).astype(jnp.float32)[:, None, None]
    kept = carry[-1] * jnp.exp(final)
    new_states = kept[:, :, None] * states + jnp.einsum('shd,shv->hdv', key_rows * tail, values, precision=highest)
    return (new_states, mixed)

def block_backward(back_after, decay_after, states, seg_before, queries, key_rows, values, decays, seg_ids, mixed_grad):
    cumul = jnp.cumsum(decays, axis=0)
    pairs, allowed = pair_decay(cumul, seg_ids)
    carry = (seg_ids == seg_before).astype(jnp.float32)
    rising = jnp.exp(cumul) * carry[:, None, None]
    final = cumul[-1]
    last_mask = (seg_ids == seg_ids[-1]).astype(jnp.float32)
    tail = jnp.exp(final[None] - cumul) * last_mask[:, None, None]
    scores = jnp.einsum('thd,shd,tshd->hts', queries, key_rows, pairs, precision=highest)
    mix_pair = jnp.einsum('thv,shv->hts', mixed_grad, values, precision=highest)
    query_vec = jnp.einsum('hts,shd,tshd->thd', mix_pair, key_rows, pairs, precision=highest)
    query_vec = query_vec + rising * jnp.einsum('thv,hdv->thd', mixed_grad, states, precision=highest)
    key_vec = jnp.einsum('hts,thd,tshd->shd', mix_pair, queries, pairs, precision=highest)
    key_vec = key_vec + tail * jnp.einsum('hdv,shv->shd', back_after, values, precision=highest)
    value_vec = jnp.einsum('hts,thv->shv', scores, mixed_grad, precision=highest)
    value_vec = value_vec + jnp.einsum('shd,hdv->shv', key_rows * tail, back_after, precision=highest)
    kept = carry[-1] * jnp.exp(final)
    back_before = jnp.einsum('thd,thv->hdv', queries * rising, mixed_grad, precision=highest) + kept[:, :, None] * back_after
    change = queries * query_vec - key_rows * key_vec
    reverse_sum = jnp.einsum('st,shd->thd', allowed, change, precision=highest)
    decay_grad = reverse_sum + last_mask[:, None, None] * decay_after[None]
    decay_before = lax.optimization_barrier(jnp.sum(carry[:, None, None] * change, axis=0)) + carry[-1] * decay_after
    return (back_before, decay_before, query_vec, key_vec, value_vec, decay_grad)

def split_blocks(array, block):
    return array.reshape((array.shape[0] // block, block) + array.shape[1:])

def join_blocks(array):
    return array.reshape((array.shape[0] * array.shape[1],) + array.shape[2:])

def mixer_forward(states, seg_before, queries, key_rows, values, decays, seg_ids, block):

    def advance(carried, pieces):
        states_in, before = carried
        query_part, key_part, value_part, decay_part, seg_part = pieces
        new_states, mixed = block_forward(states_in, before, query_part, key_part, value_part, decay_part, seg_part)
        return ((new_states, seg_part[-1]), (mixed, states_in))
    pieces = (split_blocks(queries, block), split_blocks(key_rows, block), split_blocks(values, block), split_blocks(decays, block), split_blocks(seg_ids, block))
    start = (states, jnp.reshape(seg_before, ()).astype(jnp.int32))
    (final, last_seg), (mixed, starts) = lax.scan(advance, start, pieces)
    return (final, join_blocks(mixed), starts)

def mixer_backward(back_in, decay_in, starts, seg_before, queries, key_rows, values, decays, seg_ids, mixed_grad, block):
    seg_parts = split_blocks(seg_ids, block)
    befores = jnp.concatenate([jnp.reshape(seg_before, (1,)).astype(jnp.int32), seg_parts[:-1, -1].astype(jnp.int32)])

    def retreat(carried, pieces):
        back_after, decay_after = carried
        states, before, query_part, key_part, value_part, decay_part, seg_part, grad_part = pieces
        found = block_backward(back_after, decay_after, states, before, query_part, key_part, value_part, decay_part, seg_part, grad_part)
        return ((found[0], found[1]), (found[2], found[3], found[4], found[5]))
    pieces = (starts, befores, split_blocks(queries, block), split_blocks(key_rows, block), split_blocks(values, block), split_blocks(decays, block), seg_parts, split_blocks(mixed_grad, block))
    carried, found = lax.scan(retreat, (back_in, decay_in), pieces, reverse=True)
    return (carried, (join_blocks(found[0]), join_blocks(found[1]), join_blocks(found[2]), join_blocks(found[3])))

def attn_inputs(tokens_in, attn_gain, query_weight, key_weight, value_weight, gate_weight, low_weight, rise_weight, decay_bias):
    heads = rise_weight.shape[0]
    number = tokens_in.shape[0]
    residual = tokens_in.astype(jnp.float32)
    inverse_one = inverse_rms(residual)
    normed_one = (residual * inverse_one * attn_gain.astype(jnp.float32)).astype(jnp.bfloat16)
    queries = matmul(normed_one, query_weight).astype(jnp.bfloat16).reshape(number, heads, -1)
    key_rows = matmul(normed_one, key_weight).astype(jnp.bfloat16).reshape(number, heads, -1)
    values = matmul(normed_one, value_weight).astype(jnp.bfloat16).reshape(number, heads, -1)
    gate_pre = matmul(normed_one, gate_weight).reshape(number, heads, -1)
    low_rank = matmul(normed_one, low_weight)
    rise_pre = jnp.einsum('nr,hrd->nhd', low_rank, rise_weight.astype(jnp.float32), precision=highest)
    rise_pre = rise_pre + decay_bias.astype(jnp.float32)[None]
    decays = jax.nn.log_sigmoid(rise_pre) / gate_scale
    return (residual, inverse_one, normed_one, queries, key_rows, values, gate_pre, low_rank, rise_pre, decays)

def head_output(mixed, gate_pre, head_gain):
    inverse_head = inverse_rms(mixed, head_epsilon)
    head_hat = mixed * inverse_head
    activated, slope = silu_parts(gate_pre)
    gated = (head_hat * head_gain.astype(jnp.float32) * activated).reshape(mixed.shape[0], -1).astype(jnp.bfloat16)
    return (inverse_head, head_hat, activated, slope, gated)

def ffn_forward(hidden_one, ffn_gain, ffn_gate, ffn_up):
    inverse_two = inverse_rms(hidden_one)
    normed_two = (hidden_one * inverse_two * ffn_gain.astype(jnp.float32)).astype(jnp.bfloat16)
    ffn_pre = matmul(normed_two, ffn_gate)
    ffn_lin = matmul(normed_two, ffn_up)
    ffn_silu, ffn_slope = silu_parts(ffn_pre)
    ffn_act = (ffn_silu * ffn_lin).astype(jnp.bfloat16)
    return (inverse_two, normed_two, ffn_lin, ffn_silu, ffn_slope, ffn_act)

def forward_window(tokens_in, seg_ids, states, seg_before, weights, block):
    attn_gain, query_weight, key_weight, value_weight, gate_weight, low_weight, rise_weight, decay_bias, head_gain, out_weight, ffn_gain, ffn_gate, ffn_up, ffn_down = weights
    attn_side = attn_inputs(tokens_in, attn_gain, query_weight, key_weight, value_weight, gate_weight, low_weight, rise_weight, decay_bias)
    residual, inverse_one, normed_one, queries, key_rows, values, gate_pre, low_rank, rise_pre, decays = attn_side
    final, mixed, starts = mixer_forward(states, seg_before, queries.astype(jnp.float32), key_rows.astype(jnp.float32), values.astype(jnp.float32), decays, seg_ids, block)
    head_side = head_output(mixed, gate_pre, head_gain)
    hidden_one = residual + matmul_nt(head_side[4], out_weight)
    ffn_side = ffn_forward(hidden_one, ffn_gain, ffn_gate, ffn_up)
    output = (hidden_one + matmul_nt(ffn_side[5], ffn_down)).astype(jnp.bfloat16)
    return (attn_side, final, mixed, starts, head_side, hidden_one, ffn_side, output)

def reference(tokens, segment_ids, attn_gain, query_weight, key_weight, value_weight, gate_weight, low_weight, rise_weight, decay_bias, head_gain, out_weight, ffn_gain, ffn_gate, ffn_up, ffn_down, cotangent):
    weights = (attn_gain, query_weight, key_weight, value_weight, gate_weight, low_weight, rise_weight, decay_bias, head_gain, out_weight, ffn_gain, ffn_gate, ffn_up, ffn_down)
    block = 64
    window = math.gcd(TOKENS, 4096)
    number = TOKENS // window
    token_parts = tokens.reshape(number, window, D)
    seg_parts = segment_ids.reshape(number, window)
    cot_parts = cotangent.reshape(number, window, D)
    start_states = jnp.zeros((H, DK, DV), jnp.float32)
    start_before = jnp.array(-1, jnp.int32)

    def forward_step(carried, pieces):
        states, before = carried
        tokens_in, seg_ids = pieces
        found = forward_window(tokens_in, seg_ids, states, before, weights, block)
        return ((found[1], seg_ids[-1]), (found[7], states, before))
    ignored, (outputs, window_states, window_befores) = lax.scan(forward_step, (start_states, start_before), (token_parts, seg_parts))

    def backward_step(carried, pieces):
        back_after, decay_after, grads = carried
        tokens_in, seg_ids, cotangent_in, states, before = pieces
        attn_side, final, mixed, starts, head_side, hidden_one, ffn_side, output = forward_window(tokens_in, seg_ids, states, before, weights, block)
        residual, inverse_one, normed_one, queries, key_rows, values, gate_pre, low_rank, rise_pre, decays = attn_side
        inverse_head, head_hat, activated, slope, gated = head_side
        inverse_two, normed_two, ffn_lin, ffn_silu, ffn_slope, ffn_act = ffn_side
        act_grad = matmul(cotangent_in, ffn_down)
        down_grad = matmul_tn(cotangent_in, ffn_act)
        pre_grad = (act_grad * ffn_lin * ffn_slope).astype(jnp.bfloat16)
        lin_grad = (act_grad * ffn_silu).astype(jnp.bfloat16)
        gate_two_grad = matmul_tn(normed_two, pre_grad)
        up_grad = matmul_tn(normed_two, lin_grad)
        normed_two_grad = matmul_nt(pre_grad, ffn_gate) + matmul_nt(lin_grad, ffn_up)
        ffn_gain_grad = lax.optimization_barrier(jnp.sum(normed_two_grad * hidden_one * inverse_two, axis=0))
        hidden_grad = cotangent_in.astype(jnp.float32) + norm_back(hidden_one, inverse_two, ffn_gain.astype(jnp.float32), normed_two_grad)
        hidden_low = hidden_grad.astype(jnp.bfloat16)
        out_grad = matmul_tn(hidden_low, gated)
        gated_grad = matmul(hidden_low, out_weight).reshape(mixed.shape)
        gain_head = head_gain.astype(jnp.float32)
        head_gain_grad = lax.optimization_barrier(jnp.sum(gated_grad * head_hat * activated, axis=(0, 1)))
        rows_here = mixed.shape[0]
        gate_pre_grad = (gated_grad * head_hat * gain_head * slope).reshape(rows_here, -1).astype(jnp.bfloat16)
        mixed_grad = norm_back(mixed, inverse_head, gain_head * activated, gated_grad)
        (back_before, decay_before), (query_vec, key_vec, value_vec, decay_grad) = mixer_backward(back_after, decay_after, starts, before, queries.astype(jnp.float32), key_rows.astype(jnp.float32), values.astype(jnp.float32), decays, seg_ids, mixed_grad, block)
        rise_back = decay_grad * jax.nn.sigmoid(-rise_pre) / gate_scale
        bias_grad = lax.optimization_barrier(jnp.sum(rise_back, axis=0))
        rise_grad = jnp.einsum('nr,nhd->hrd', low_rank, rise_back, precision=highest)
        low_back = jnp.einsum('nhd,hrd->nr', rise_back, rise_weight.astype(jnp.float32), precision=highest).astype(jnp.bfloat16)
        query_back = query_vec.reshape(rows_here, -1).astype(jnp.bfloat16)
        key_back = key_vec.reshape(rows_here, -1).astype(jnp.bfloat16)
        value_back = value_vec.reshape(rows_here, -1).astype(jnp.bfloat16)
        query_grad = matmul_tn(normed_one, query_back)
        key_grad = matmul_tn(normed_one, key_back)
        value_grad = matmul_tn(normed_one, value_back)
        gate_grad = matmul_tn(normed_one, gate_pre_grad)
        low_grad = matmul_tn(normed_one, low_back)
        normed_one_grad = matmul_nt(query_back, query_weight) + matmul_nt(key_back, key_weight) + matmul_nt(value_back, value_weight) + matmul_nt(gate_pre_grad, gate_weight) + matmul_nt(low_back, low_weight)
        attn_gain_grad = lax.optimization_barrier(jnp.sum(normed_one_grad * residual * inverse_one, axis=0))
        tokens_grad = hidden_grad + norm_back(residual, inverse_one, attn_gain.astype(jnp.float32), normed_one_grad)
        fresh = (attn_gain_grad, query_grad, key_grad, value_grad, gate_grad, low_grad, rise_grad, bias_grad, head_gain_grad, out_grad, ffn_gain_grad, gate_two_grad, up_grad, down_grad)
        summed = tuple((older + newer for older, newer in zip(grads, fresh)))
        return ((back_before, decay_before, summed), tokens_grad)
    zero_grads = tuple((jnp.zeros(weight.shape, jnp.float32) for weight in weights))
    start = (jnp.zeros((H, DK, DV), jnp.float32), jnp.zeros((H, DK), jnp.float32), zero_grads)
    (back_end, decay_end, grads), token_grads = lax.scan(backward_step, start, (token_parts, seg_parts, cot_parts, window_states, window_befores), reverse=True)
    return (outputs.reshape(TOKENS, D), token_grads.reshape(TOKENS, D), grads[0], grads[1], grads[2], grads[3], grads[4], grads[5], grads[6], grads[7], grads[8], grads[9], grads[10], grads[11], grads[12], grads[13])
```

```python
import jax
import jax.numpy as jnp
from jax import lax
from jax.sharding import PartitionSpec as P

epsilon = 1e-06
head_epsilon = 1.0
gate_scale = 16.0
longest = 512
lanes = 128
other_core = [(0, 1), (1, 0)]
highest = lax.Precision.HIGHEST


def passed_along(shard, axis, by):
    count = lax.axis_size(axis)
    pairs = [(i, i + by) for i in range(count) if 0 <= i + by < count]
    return lax.ppermute(shard, axis, pairs)


def hop_count(local):
    return -(-(longest - 1) // local)


def keeps_nearby(keep, axis, reverse, hops):
    step = -1 if reverse else 1
    return [passed_along(keep, axis, step * hop) for hop in range(1, hops)]


def entering(keeps, part, axis, reverse):
    step = -1 if reverse else 1
    hops = len(keeps) + 1
    parts = [passed_along(part, axis, step * hop) for hop in range(1, hops + 1)]
    state = parts[-1]
    for hop in range(hops - 2, -1, -1):
        keep = keeps[hop]
        state = parts[hop] + keep.reshape(keep.shape + (1,) * (part.ndim - keep.ndim)) * state
    return state


def pair_sum(part):
    return part + lax.ppermute(part, "tensor", other_core)


def matmul(left, right):
    return jnp.dot(left, right, preferred_element_type=jnp.float32)


def matmul_nt(left, right):
    return lax.dot_general(
        left, right, (((1,), (1,)), ((), ())), preferred_element_type=jnp.float32
    )


def matmul_tn(left, right):
    return lax.dot_general(
        left, right, (((0,), (0,)), ((), ())), preferred_element_type=jnp.float32
    )


def inverse_rms(entries, small=epsilon):
    return lax.rsqrt(jnp.mean(entries * entries, axis=-1, keepdims=True) + small)


def norm_back(entries, inverse, scale_by, grad):
    scaled = grad * scale_by
    return inverse * scaled - entries * inverse**3 * jnp.mean(
        scaled * entries, axis=-1, keepdims=True
    )


def silu_parts(pre_act):
    logistic = jax.nn.sigmoid(pre_act)
    return (pre_act * logistic, logistic * (1.0 + pre_act * (1.0 - logistic)))


def pair_decay(cumul, seg_ids):
    places = jnp.arange(seg_ids.shape[0])
    allowed = (
        (places[:, None] >= places[None, :]) & (seg_ids[:, None] == seg_ids[None, :])
    ).astype(jnp.float32)
    spread = jnp.minimum(cumul[:, None] - cumul[None, :], 0.0)
    return (jnp.exp(spread) * allowed[:, :, None, None], allowed)


def block_forward(states, seg_before, queries, key_rows, values, decays, seg_ids):
    cumul = jnp.cumsum(decays, axis=0)
    pairs, allowed = pair_decay(cumul, seg_ids)
    carry = (seg_ids == seg_before).astype(jnp.float32)
    scores = jnp.einsum("thd,shd,tshd->hts", queries, key_rows, pairs, precision=highest)
    mixed = jnp.einsum("hts,shv->thv", scores, values, precision=highest)
    rising = jnp.exp(cumul) * carry[:, None, None]
    mixed = mixed + jnp.einsum("thd,hdv->thv", queries * rising, states, precision=highest)
    final = cumul[-1]
    tail = (
        jnp.exp(final[None] - cumul) * (seg_ids == seg_ids[-1]).astype(jnp.float32)[:, None, None]
    )
    kept = carry[-1] * jnp.exp(final)
    new_states = kept[:, :, None] * states + jnp.einsum(
        "shd,shv->hdv", key_rows * tail, values, precision=highest
    )
    return (new_states, mixed)


def block_backward(
    back_after,
    decay_after,
    states,
    seg_before,
    queries,
    key_rows,
    values,
    decays,
    seg_ids,
    mixed_grad,
):
    cumul = jnp.cumsum(decays, axis=0)
    pairs, allowed = pair_decay(cumul, seg_ids)
    carry = (seg_ids == seg_before).astype(jnp.float32)
    rising = jnp.exp(cumul) * carry[:, None, None]
    final = cumul[-1]
    last_mask = (seg_ids == seg_ids[-1]).astype(jnp.float32)
    tail = jnp.exp(final[None] - cumul) * last_mask[:, None, None]
    scores = jnp.einsum("thd,shd,tshd->hts", queries, key_rows, pairs, precision=highest)
    mix_pair = jnp.einsum("thv,shv->hts", mixed_grad, values, precision=highest)
    query_vec = jnp.einsum("hts,shd,tshd->thd", mix_pair, key_rows, pairs, precision=highest)
    query_vec = query_vec + rising * jnp.einsum(
        "thv,hdv->thd", mixed_grad, states, precision=highest
    )
    key_vec = jnp.einsum("hts,thd,tshd->shd", mix_pair, queries, pairs, precision=highest)
    key_vec = key_vec + tail * jnp.einsum("hdv,shv->shd", back_after, values, precision=highest)
    value_vec = jnp.einsum("hts,thv->shv", scores, mixed_grad, precision=highest)
    value_vec = value_vec + jnp.einsum(
        "shd,hdv->shv", key_rows * tail, back_after, precision=highest
    )
    kept = carry[-1] * jnp.exp(final)
    back_before = (
        jnp.einsum("thd,thv->hdv", queries * rising, mixed_grad, precision=highest)
        + kept[:, :, None] * back_after
    )
    change = queries * query_vec - key_rows * key_vec
    reverse_sum = jnp.einsum("st,shd->thd", allowed, change, precision=highest)
    decay_grad = reverse_sum + last_mask[:, None, None] * decay_after[None]
    decay_before = jnp.sum(carry[:, None, None] * change, axis=0) + carry[-1] * decay_after
    return (back_before, decay_before, query_vec, key_vec, value_vec, decay_grad)


def split_blocks(array, block):
    return array.reshape((array.shape[0] // block, block) + array.shape[1:])


def join_blocks(array):
    return array.reshape((array.shape[0] * array.shape[1],) + array.shape[2:])


def mixer_forward(states, seg_before, queries, key_rows, values, decays, seg_ids, block):

    def advance(carried, pieces):
        states_in, before = carried
        query_part, key_part, value_part, decay_part, seg_part = pieces
        new_states, mixed = block_forward(
            states_in, before, query_part, key_part, value_part, decay_part, seg_part
        )
        return ((new_states, seg_part[-1]), (mixed, states_in))

    pieces = (
        split_blocks(queries, block),
        split_blocks(key_rows, block),
        split_blocks(values, block),
        split_blocks(decays, block),
        split_blocks(seg_ids, block),
    )
    start = (states, seg_before)
    (final, last_seg), (mixed, starts) = lax.scan(advance, start, pieces)
    return (final, join_blocks(mixed), starts)


def mixer_backward(
    back_in,
    decay_in,
    starts,
    seg_before,
    queries,
    key_rows,
    values,
    decays,
    seg_ids,
    mixed_grad,
    block,
):
    seg_parts = split_blocks(seg_ids, block)
    befores = jnp.concatenate([jnp.reshape(seg_before, (1,)), seg_parts[:-1, -1]])

    def retreat(carried, pieces):
        back_after, decay_after = carried
        states, before, query_part, key_part, value_part, decay_part, seg_part, grad_part = pieces
        found = block_backward(
            back_after,
            decay_after,
            states,
            before,
            query_part,
            key_part,
            value_part,
            decay_part,
            seg_part,
            grad_part,
        )
        return ((found[0], found[1]), (found[2], found[3], found[4], found[5]))

    pieces = (
        starts,
        befores,
        split_blocks(queries, block),
        split_blocks(key_rows, block),
        split_blocks(values, block),
        split_blocks(decays, block),
        seg_parts,
        split_blocks(mixed_grad, block),
    )
    carried, found = lax.scan(retreat, (back_in, decay_in), pieces, reverse=True)
    return (
        carried,
        (
            join_blocks(found[0]),
            join_blocks(found[1]),
            join_blocks(found[2]),
            join_blocks(found[3]),
        ),
    )


def head_output(mixed, gate_pre, head_gain):
    inverse_head = inverse_rms(mixed, head_epsilon)
    head_hat = mixed * inverse_head
    activated, slope = silu_parts(gate_pre)
    gated = (
        (head_hat * head_gain * activated)
        .reshape(mixed.shape[0], -1)
        .astype(jnp.bfloat16)
    )
    return (inverse_head, head_hat, activated, slope, gated)


def ffn_forward(hidden_one, ffn_gain, ffn_gate, ffn_up):
    inverse_two = inverse_rms(hidden_one)
    normed_two = (hidden_one * inverse_two * ffn_gain.astype(jnp.float32)).astype(jnp.bfloat16)
    ffn_pre = matmul(normed_two, ffn_gate)
    ffn_lin = matmul(normed_two, ffn_up)
    ffn_silu, ffn_slope = silu_parts(ffn_pre)
    ffn_act = (ffn_silu * ffn_lin).astype(jnp.bfloat16)
    return (inverse_two, normed_two, ffn_lin, ffn_silu, ffn_slope, ffn_act)


def body(
    tokens,
    segment_ids,
    attn_gain,
    query_weight,
    key_weight,
    value_weight,
    gate_weight,
    low_weight,
    rise_weight,
    decay_bias,
    head_gain,
    out_weight,
    ffn_gain,
    ffn_gate,
    ffn_up,
    ffn_down,
    cotangent,
):
    f32, bf16 = jnp.float32, jnp.bfloat16
    count = lax.axis_size("dp")
    place = lax.axis_index("dp")
    local = tokens.shape[0]
    block = min(64, local)
    hops = min(hop_count(local), count - 1)
    rows = query_weight.shape[0]
    heads, rank, dk_own = rise_weight.shape
    dv_own = head_gain.shape[0]
    cuts = [query_weight.shape[1], key_weight.shape[1], value_weight.shape[1], gate_weight.shape[1]]
    ends = [sum(cuts[: i + 1]) for i in range(4)]
    width = ends[3]
    units = ffn_gate.shape[1]
    rise_size, bias_size = heads * rank * dk_own, heads * dk_own
    tiny = jnp.concatenate(
        [
            rise_weight.reshape(-1),
            decay_bias.reshape(-1),
            head_gain,
            segment_ids[local - 1 :].astype(bf16),
        ]
    )
    tiny_size = tiny.shape[0]
    tiny_columns = -(-tiny_size // rows)
    used = rank + 2 + tiny_columns
    extra_width = -(-used // lanes) * lanes
    tiny = jnp.pad(tiny, (0, tiny_columns * rows - tiny_size)).reshape(rows, tiny_columns)
    extra = jnp.concatenate(
        [
            low_weight,
            attn_gain[:, None],
            ffn_gain[:, None],
            tiny,
            jnp.zeros((rows, extra_width - used), bf16),
        ],
        axis=1,
    )
    attn_pack = jnp.concatenate(
        [query_weight, key_weight, value_weight, gate_weight, extra, out_weight], axis=1
    )
    attn_all = lax.all_gather(attn_pack, "dp", axis=0, tiled=True)
    ffn_pack = jnp.concatenate([ffn_gate, ffn_up, ffn_down], axis=1)
    ffn_all = lax.all_gather(ffn_pack, "dp", axis=0, tiled=True)

    full_in = attn_all[:, : width + extra_width]
    full_proj = attn_all[:, :width]
    full_extra = attn_all[:, width : width + extra_width]
    full_out = attn_all[:, width + extra_width :]
    full_low = full_extra[:, :rank]
    full_attn_gain = full_extra[:, rank].astype(f32)
    full_ffn_gain = full_extra[:, rank + 1].astype(f32)
    tinies = full_extra[:, rank + 2 : used].reshape(count, tiny_columns * rows)
    full_rise = (
        tinies[:, :rise_size]
        .reshape(count, heads, rank, dk_own)
        .transpose(1, 2, 0, 3)
        .reshape(heads, rank, -1)
        .astype(f32)
    )
    full_bias = (
        tinies[:, rise_size : rise_size + bias_size]
        .reshape(count, heads, dk_own)
        .transpose(1, 0, 2)
        .reshape(heads, -1)
        .astype(f32)
    )
    start = rise_size + bias_size
    full_head_gain = tinies[:, start : start + dv_own].reshape(-1).astype(f32)
    last_ids = tinies[:, start + dv_own].astype(jnp.int32)
    seg_before = jnp.where(
        place > 0, lax.dynamic_index_in_dim(last_ids, jnp.maximum(place - 1, 0), 0, False), -1
    )

    residual = tokens.astype(f32)
    inverse_one = inverse_rms(residual)
    normed_one = (residual * inverse_one * full_attn_gain).astype(bf16)
    projected = matmul(normed_one, full_in)
    queries = projected[:, : ends[0]].astype(bf16).reshape(local, heads, -1)
    key_rows = projected[:, ends[0] : ends[1]].astype(bf16).reshape(local, heads, -1)
    values = projected[:, ends[1] : ends[2]].astype(bf16).reshape(local, heads, -1)
    gate_pre = projected[:, ends[2] : ends[3]].reshape(local, heads, -1)
    low_rank = projected[:, width : width + rank]
    rise_pre = jnp.einsum("nr,hrd->nhd", low_rank, full_rise, precision=highest) + full_bias[None]
    decays = jax.nn.log_sigmoid(rise_pre) / gate_scale

    query_f = queries.astype(f32)
    key_f = key_rows.astype(f32)
    value_f = values.astype(f32)
    cumul = jnp.cumsum(decays, axis=0)
    total = cumul[-1]
    joined = (segment_ids[local - 1] == seg_before).astype(f32)
    whole_keep = joined * jnp.exp(total)
    last_mask = (segment_ids == segment_ids[local - 1]).astype(f32)
    tail = jnp.exp(total[None] - cumul) * last_mask[:, None, None]
    keeps_before = keeps_nearby(whole_keep, "dp", False, hops)
    keeps_after = keeps_nearby(whole_keep, "dp", True, hops)
    local_state = jnp.einsum("shd,shv->hdv", key_f * tail, value_f, precision=highest)
    incoming = entering(keeps_before, local_state, "dp", False)
    final, mixed, starts = mixer_forward(
        incoming, seg_before, query_f, key_f, value_f, decays, segment_ids, block
    )
    inverse_head, head_hat, activated, slope, gated = head_output(mixed, gate_pre, full_head_gain)
    attn_total = pair_sum(matmul_nt(gated, full_out))
    hidden_one = residual + attn_total
    inverse_two = inverse_rms(hidden_one)
    normed_two = (hidden_one * inverse_two * full_ffn_gain).astype(bf16)
    full_up_pair = ffn_all[:, : 2 * units]
    full_down = ffn_all[:, 2 * units :]
    ffn_both = matmul(normed_two, full_up_pair)
    ffn_pre, ffn_lin = ffn_both[:, :units], ffn_both[:, units:]
    ffn_silu, ffn_slope = silu_parts(ffn_pre)
    ffn_act = (ffn_silu * ffn_lin).astype(bf16)
    ffn_total = pair_sum(matmul_nt(ffn_act, full_down))
    output = (hidden_one + ffn_total).astype(bf16)

    act_grad = matmul(cotangent, full_down)
    down_grad = matmul_tn(cotangent, ffn_act).astype(bf16)
    pre_grad = (act_grad * ffn_lin * ffn_slope).astype(bf16)
    lin_grad = (act_grad * ffn_silu).astype(bf16)
    both_grad = jnp.concatenate([pre_grad, lin_grad], axis=1)
    up_pair_grad = matmul_tn(normed_two, both_grad).astype(bf16)
    normed_two_grad = pair_sum(matmul_nt(both_grad, full_up_pair))
    ffn_gain_grad = jnp.sum(normed_two_grad * hidden_one * inverse_two, axis=0)
    hidden_grad = cotangent.astype(f32) + norm_back(
        hidden_one, inverse_two, full_ffn_gain, normed_two_grad
    )
    hidden_low = hidden_grad.astype(bf16)
    out_grad = matmul_tn(hidden_low, gated).astype(bf16)
    ffn_sums = lax.psum_scatter(
        jnp.concatenate([up_pair_grad, down_grad, out_grad], axis=1),
        "dp",
        scatter_dimension=0,
        tiled=True,
    ).astype(f32)
    gated_grad = matmul(hidden_low, full_out).reshape(mixed.shape)
    head_gain_part = pair_sum(jnp.sum(gated_grad * head_hat * activated, axis=(0, 1)))
    gate_pre_grad = (
        (gated_grad * head_hat * full_head_gain * slope).reshape(local, -1).astype(bf16)
    )
    mixed_grad = norm_back(mixed, inverse_head, full_head_gain * activated, gated_grad)
    rising = jnp.exp(cumul) * (segment_ids == seg_before).astype(f32)[:, None, None]
    local_back = jnp.einsum("thd,thv->hdv", query_f * rising, mixed_grad, precision=highest)
    back_in = entering(keeps_after, local_back, "dp", True)
    carried, found = mixer_backward(
        back_in,
        jnp.zeros_like(total),
        starts,
        seg_before,
        query_f,
        key_f,
        value_f,
        decays,
        segment_ids,
        mixed_grad,
        block,
    )
    query_vec, key_vec, value_vec, decay_local = found
    joined_after = []
    for hop in range(1, hops):
        at = jnp.minimum(place + hop, count - 1)
        same = lax.dynamic_index_in_dim(last_ids, at, 0, False) == lax.dynamic_index_in_dim(
            last_ids, at - 1, 0, False
        )
        joined_after.append((same & (place + hop < count)).astype(f32))
    decay_in = entering(joined_after, carried[1], "dp", True)
    decay_grad = decay_local + last_mask[:, None, None] * decay_in[None]
    rise_back = decay_grad * jax.nn.sigmoid(-rise_pre) / gate_scale
    bias_grad = jnp.sum(rise_back, axis=0)
    rise_grad = jnp.einsum("nr,nhd->hrd", low_rank, rise_back, precision=highest)
    proj_back = jnp.concatenate(
        [
            query_vec.reshape(local, -1).astype(bf16),
            key_vec.reshape(local, -1).astype(bf16),
            value_vec.reshape(local, -1).astype(bf16),
            gate_pre_grad,
        ],
        axis=1,
    )
    proj_grad = matmul_tn(normed_one, proj_back).astype(bf16)
    low_back = pair_sum(
        jnp.einsum("nhd,hrd->nr", rise_back, full_rise, precision=highest)
    ).astype(bf16)
    normed_one_grad = pair_sum(matmul_nt(proj_back, full_proj)) + matmul_nt(low_back, full_low)
    low_grad = matmul_tn(normed_one, low_back).astype(bf16)
    attn_gain_grad = jnp.sum(normed_one_grad * residual * inverse_one, axis=0)
    tokens_grad = hidden_grad + norm_back(residual, inverse_one, full_attn_gain, normed_one_grad)
    tiny_grad = jnp.concatenate(
        [
            rise_grad.reshape(heads, rank, count, dk_own).transpose(2, 0, 1, 3).reshape(count, -1),
            bias_grad.reshape(heads, count, dk_own).transpose(1, 0, 2).reshape(count, -1),
            head_gain_part.reshape(count, dv_own),
        ],
        axis=1,
    )
    tiny_grad = jnp.pad(tiny_grad, ((0, 0), (0, tiny_columns * rows - tiny_size + 1)))
    attn_sums = lax.psum_scatter(
        jnp.concatenate(
            [
                proj_grad,
                low_grad,
                attn_gain_grad[:, None].astype(bf16),
                ffn_gain_grad[:, None].astype(bf16),
                tiny_grad.reshape(count * rows, tiny_columns).astype(bf16),
                jnp.zeros((count * rows, extra_width - used), bf16),
            ],
            axis=1,
        ),
        "dp",
        scatter_dimension=0,
        tiled=True,
    ).astype(f32)
    tiny_sums = attn_sums[:, width + rank + 2 : width + used].reshape(-1)
    return (
        output,
        tokens_grad,
        attn_sums[:, width + rank],
        attn_sums[:, : ends[0]],
        attn_sums[:, ends[0] : ends[1]],
        attn_sums[:, ends[1] : ends[2]],
        attn_sums[:, ends[2] : ends[3]],
        attn_sums[:, width : width + rank],
        tiny_sums[:rise_size].reshape(heads, rank, dk_own),
        tiny_sums[rise_size : rise_size + bias_size].reshape(heads, dk_own),
        tiny_sums[start : start + dv_own],
        ffn_sums[:, 3 * units :],
        attn_sums[:, width + rank + 1],
        ffn_sums[:, :units],
        ffn_sums[:, units : 2 * units],
        ffn_sums[:, 2 * units : 3 * units],
    )


def solution(mesh):
    return jax.shard_map(
        body,
        mesh=mesh,
        in_specs=(
            P("dp", None),
            P("dp"),
            P("dp"),
            P("dp", "tensor"),
            P("dp", "tensor"),
            P("dp", "tensor"),
            P("dp", "tensor"),
            P("dp", None),
            P("tensor", None, "dp"),
            P("tensor", "dp"),
            P("dp"),
            P("dp", "tensor"),
            P("dp"),
            P("dp", "tensor"),
            P("dp", "tensor"),
            P("dp", "tensor"),
            P("dp", None),
        ),
        out_specs=(
            P("dp", None),
            P("dp", None),
            P("dp"),
            P("dp", "tensor"),
            P("dp", "tensor"),
            P("dp", "tensor"),
            P("dp", "tensor"),
            P("dp", None),
            P("tensor", None, "dp"),
            P("tensor", "dp"),
            P("dp"),
            P("dp", "tensor"),
            P("dp"),
            P("dp", "tensor"),
            P("dp", "tensor"),
            P("dp", "tensor"),
        ),
        check_vma=False,
    )
```

```python
import jax
import jax.numpy as jnp
from jax import lax
from jax.sharding import PartitionSpec as P

epsilon = 1e-06
head_epsilon = 1.0
gate_scale = 16.0
longest = 512
lanes = 128
other_core = [(0, 1), (1, 0)]
highest = lax.Precision.HIGHEST


def passed_along(shard, axis, by):
    count = lax.axis_size(axis)
    pairs = [(i, i + by) for i in range(count) if 0 <= i + by < count]
    return lax.ppermute(shard, axis, pairs)


def hop_count(local):
    return -(-(longest - 1) // local)


def keeps_nearby(keep, axis, reverse, hops):
    step = -1 if reverse else 1
    return [passed_along(keep, axis, step * hop) for hop in range(1, hops)]


def entering(keeps, part, axis, reverse, sent=jnp.float32):
    step = -1 if reverse else 1
    hops = len(keeps) + 1
    parts = [
        passed_along(part.astype(sent), axis, step * hop).astype(jnp.float32)
        for hop in range(1, hops + 1)
    ]
    state = parts[-1]
    for hop in range(hops - 2, -1, -1):
        keep = keeps[hop]
        state = parts[hop] + keep.reshape(keep.shape + (1,) * (part.ndim - keep.ndim)) * state
    return state


def pair_sum(part):
    return part + lax.ppermute(part, "tensor", other_core)


def matmul(left, right):
    return jnp.dot(left, right, preferred_element_type=jnp.float32)


def matmul_nt(left, right):
    return lax.dot_general(
        left, right, (((1,), (1,)), ((), ())), preferred_element_type=jnp.float32
    )


def matmul_tn(left, right):
    return lax.dot_general(
        left, right, (((0,), (0,)), ((), ())), preferred_element_type=jnp.float32
    )


def inverse_rms(entries, small=epsilon):
    return lax.rsqrt(jnp.mean(entries * entries, axis=-1, keepdims=True) + small)


def norm_back(entries, inverse, scale_by, grad):
    scaled = grad * scale_by
    return inverse * scaled - entries * inverse**3 * jnp.mean(
        scaled * entries, axis=-1, keepdims=True
    )


def silu_parts(pre_act):
    logistic = jax.nn.sigmoid(pre_act)
    return (pre_act * logistic, logistic * (1.0 + pre_act * (1.0 - logistic)))


def pair_decay(cumul, seg_ids):
    places = jnp.arange(seg_ids.shape[0])
    allowed = (
        (places[:, None] >= places[None, :]) & (seg_ids[:, None] == seg_ids[None, :])
    ).astype(jnp.float32)
    spread = jnp.minimum(cumul[:, None] - cumul[None, :], 0.0)
    return (jnp.exp(spread) * allowed[:, :, None, None], allowed)


def block_forward(states, seg_before, queries, key_rows, values, decays, seg_ids):
    cumul = jnp.cumsum(decays, axis=0)
    pairs, allowed = pair_decay(cumul, seg_ids)
    carry = (seg_ids == seg_before).astype(jnp.float32)
    scores = jnp.einsum("thd,shd,tshd->hts", queries, key_rows, pairs, precision=highest)
    mixed = jnp.einsum("hts,shv->thv", scores, values, precision=highest)
    rising = jnp.exp(cumul) * carry[:, None, None]
    mixed = mixed + jnp.einsum("thd,hdv->thv", queries * rising, states, precision=highest)
    final = cumul[-1]
    tail = (
        jnp.exp(final[None] - cumul) * (seg_ids == seg_ids[-1]).astype(jnp.float32)[:, None, None]
    )
    kept = carry[-1] * jnp.exp(final)
    new_states = kept[:, :, None] * states + jnp.einsum(
        "shd,shv->hdv", key_rows * tail, values, precision=highest
    )
    return (new_states, mixed)


def block_backward(
    back_after,
    decay_after,
    states,
    seg_before,
    queries,
    key_rows,
    values,
    decays,
    seg_ids,
    mixed_grad,
):
    cumul = jnp.cumsum(decays, axis=0)
    pairs, allowed = pair_decay(cumul, seg_ids)
    carry = (seg_ids == seg_before).astype(jnp.float32)
    rising = jnp.exp(cumul) * carry[:, None, None]
    final = cumul[-1]
    last_mask = (seg_ids == seg_ids[-1]).astype(jnp.float32)
    tail = jnp.exp(final[None] - cumul) * last_mask[:, None, None]
    scores = jnp.einsum("thd,shd,tshd->hts", queries, key_rows, pairs, precision=highest)
    mix_pair = jnp.einsum("thv,shv->hts", mixed_grad, values, precision=highest)
    query_vec = jnp.einsum("hts,shd,tshd->thd", mix_pair, key_rows, pairs, precision=highest)
    query_vec = query_vec + rising * jnp.einsum(
        "thv,hdv->thd", mixed_grad, states, precision=highest
    )
    key_vec = jnp.einsum("hts,thd,tshd->shd", mix_pair, queries, pairs, precision=highest)
    key_vec = key_vec + tail * jnp.einsum("hdv,shv->shd", back_after, values, precision=highest)
    value_vec = jnp.einsum("hts,thv->shv", scores, mixed_grad, precision=highest)
    value_vec = value_vec + jnp.einsum(
        "shd,hdv->shv", key_rows * tail, back_after, precision=highest
    )
    kept = carry[-1] * jnp.exp(final)
    back_before = (
        jnp.einsum("thd,thv->hdv", queries * rising, mixed_grad, precision=highest)
        + kept[:, :, None] * back_after
    )
    change = queries * query_vec - key_rows * key_vec
    reverse_sum = jnp.einsum("st,shd->thd", allowed, change, precision=highest)
    decay_grad = reverse_sum + last_mask[:, None, None] * decay_after[None]
    decay_before = jnp.sum(carry[:, None, None] * change, axis=0) + carry[-1] * decay_after
    return (back_before, decay_before, query_vec, key_vec, value_vec, decay_grad)


def split_blocks(array, block):
    return array.reshape((array.shape[0] // block, block) + array.shape[1:])


def join_blocks(array):
    return array.reshape((array.shape[0] * array.shape[1],) + array.shape[2:])


def mixer_forward(states, seg_before, queries, key_rows, values, decays, seg_ids, block):

    def advance(carried, pieces):
        states_in, before = carried
        query_part, key_part, value_part, decay_part, seg_part = pieces
        new_states, mixed = block_forward(
            states_in, before, query_part, key_part, value_part, decay_part, seg_part
        )
        return ((new_states, seg_part[-1]), (mixed, states_in))

    pieces = (
        split_blocks(queries, block),
        split_blocks(key_rows, block),
        split_blocks(values, block),
        split_blocks(decays, block),
        split_blocks(seg_ids, block),
    )
    start = (states, seg_before)
    (final, last_seg), (mixed, starts) = lax.scan(advance, start, pieces)
    return (final, join_blocks(mixed), starts)


def mixer_backward(
    back_in,
    decay_in,
    starts,
    seg_before,
    queries,
    key_rows,
    values,
    decays,
    seg_ids,
    mixed_grad,
    block,
):
    seg_parts = split_blocks(seg_ids, block)
    befores = jnp.concatenate([jnp.reshape(seg_before, (1,)), seg_parts[:-1, -1]])

    def retreat(carried, pieces):
        back_after, decay_after = carried
        states, before, query_part, key_part, value_part, decay_part, seg_part, grad_part = pieces
        found = block_backward(
            back_after,
            decay_after,
            states,
            before,
            query_part,
            key_part,
            value_part,
            decay_part,
            seg_part,
            grad_part,
        )
        return ((found[0], found[1]), (found[2], found[3], found[4], found[5]))

    pieces = (
        starts,
        befores,
        split_blocks(queries, block),
        split_blocks(key_rows, block),
        split_blocks(values, block),
        split_blocks(decays, block),
        seg_parts,
        split_blocks(mixed_grad, block),
    )
    carried, found = lax.scan(retreat, (back_in, decay_in), pieces, reverse=True)
    return (
        carried,
        (
            join_blocks(found[0]),
            join_blocks(found[1]),
            join_blocks(found[2]),
            join_blocks(found[3]),
        ),
    )


def head_output(mixed, gate_pre, head_gain):
    inverse_head = inverse_rms(mixed, head_epsilon)
    head_hat = mixed * inverse_head
    activated, slope = silu_parts(gate_pre)
    gated = (
        (head_hat * head_gain * activated)
        .reshape(mixed.shape[0], -1)
        .astype(jnp.bfloat16)
    )
    return (inverse_head, head_hat, activated, slope, gated)


def ffn_forward(hidden_one, ffn_gain, ffn_gate, ffn_up):
    inverse_two = inverse_rms(hidden_one)
    normed_two = (hidden_one * inverse_two * ffn_gain.astype(jnp.float32)).astype(jnp.bfloat16)
    ffn_pre = matmul(normed_two, ffn_gate)
    ffn_lin = matmul(normed_two, ffn_up)
    ffn_silu, ffn_slope = silu_parts(ffn_pre)
    ffn_act = (ffn_silu * ffn_lin).astype(jnp.bfloat16)
    return (inverse_two, normed_two, ffn_lin, ffn_silu, ffn_slope, ffn_act)


def body(
    tokens,
    segment_ids,
    attn_gain,
    query_weight,
    key_weight,
    value_weight,
    gate_weight,
    low_weight,
    rise_weight,
    decay_bias,
    head_gain,
    out_weight,
    ffn_gain,
    ffn_gate,
    ffn_up,
    ffn_down,
    cotangent,
):
    f32, bf16 = jnp.float32, jnp.bfloat16
    count = lax.axis_size("dp")
    place = lax.axis_index("dp")
    local = tokens.shape[0]
    block = min(64, local)
    hops = min(hop_count(local), count - 1)
    rows = query_weight.shape[0]
    heads, rank, dk_own = rise_weight.shape
    dv_own = head_gain.shape[0]
    cuts = [query_weight.shape[1], key_weight.shape[1], value_weight.shape[1], gate_weight.shape[1]]
    ends = [sum(cuts[: i + 1]) for i in range(4)]
    width = ends[3]
    units = ffn_gate.shape[1]
    rise_size, bias_size = heads * rank * dk_own, heads * dk_own
    tiny = jnp.concatenate(
        [
            rise_weight.reshape(-1),
            decay_bias.reshape(-1),
            head_gain,
            segment_ids[local - 1 :].astype(bf16),
        ]
    )
    tiny_size = tiny.shape[0]
    tiny_columns = -(-tiny_size // rows)
    used = rank + 2 + tiny_columns
    extra_width = -(-used // lanes) * lanes
    tiny = jnp.pad(tiny, (0, tiny_columns * rows - tiny_size)).reshape(rows, tiny_columns)
    extra = jnp.concatenate(
        [
            low_weight,
            attn_gain[:, None],
            ffn_gain[:, None],
            tiny,
            jnp.zeros((rows, extra_width - used), bf16),
        ],
        axis=1,
    )
    attn_pack = jnp.concatenate(
        [query_weight, key_weight, value_weight, gate_weight, extra, out_weight], axis=1
    )
    attn_all = lax.all_gather(attn_pack, "dp", axis=0, tiled=True)
    ffn_pack = jnp.concatenate([ffn_gate, ffn_up, ffn_down], axis=1)
    ffn_all = lax.all_gather(ffn_pack, "dp", axis=0, tiled=True)

    full_in = attn_all[:, : width + extra_width]
    full_proj = attn_all[:, :width]
    full_extra = attn_all[:, width : width + extra_width]
    full_out = attn_all[:, width + extra_width :]
    full_low = full_extra[:, :rank]
    full_attn_gain = full_extra[:, rank].astype(f32)
    full_ffn_gain = full_extra[:, rank + 1].astype(f32)
    tinies = full_extra[:, rank + 2 : used].reshape(count, tiny_columns * rows)
    full_rise = (
        tinies[:, :rise_size]
        .reshape(count, heads, rank, dk_own)
        .transpose(1, 2, 0, 3)
        .reshape(heads, rank, -1)
        .astype(f32)
    )
    full_bias = (
        tinies[:, rise_size : rise_size + bias_size]
        .reshape(count, heads, dk_own)
        .transpose(1, 0, 2)
        .reshape(heads, -1)
        .astype(f32)
    )
    start = rise_size + bias_size
    full_head_gain = tinies[:, start : start + dv_own].reshape(-1).astype(f32)
    last_ids = tinies[:, start + dv_own].astype(jnp.int32)
    seg_before = jnp.where(
        place > 0, lax.dynamic_index_in_dim(last_ids, jnp.maximum(place - 1, 0), 0, False), -1
    )

    residual = tokens.astype(f32)
    inverse_one = inverse_rms(residual)
    normed_one = (residual * inverse_one * full_attn_gain).astype(bf16)
    projected = matmul(normed_one, full_in)
    queries = projected[:, : ends[0]].astype(bf16).reshape(local, heads, -1)
    key_rows = projected[:, ends[0] : ends[1]].astype(bf16).reshape(local, heads, -1)
    values = projected[:, ends[1] : ends[2]].astype(bf16).reshape(local, heads, -1)
    gate_pre = projected[:, ends[2] : ends[3]].reshape(local, heads, -1)
    low_rank = projected[:, width : width + rank]
    rise_pre = jnp.einsum("nr,hrd->nhd", low_rank, full_rise, precision=highest) + full_bias[None]
    decays = jax.nn.log_sigmoid(rise_pre) / gate_scale

    query_f = queries.astype(f32)
    key_f = key_rows.astype(f32)
    value_f = values.astype(f32)
    cumul = jnp.cumsum(decays, axis=0)
    total = cumul[-1]
    joined = (segment_ids[local - 1] == seg_before).astype(f32)
    whole_keep = joined * jnp.exp(total)
    last_mask = (segment_ids == segment_ids[local - 1]).astype(f32)
    tail = jnp.exp(total[None] - cumul) * last_mask[:, None, None]
    keeps_before = keeps_nearby(whole_keep, "dp", False, hops)
    keeps_after = keeps_nearby(whole_keep, "dp", True, hops)
    local_state = jnp.einsum("shd,shv->hdv", key_f * tail, value_f, precision=highest)
    incoming = entering(keeps_before, local_state, "dp", False, bf16)
    final, mixed, starts = mixer_forward(
        incoming, seg_before, query_f, key_f, value_f, decays, segment_ids, block
    )
    inverse_head, head_hat, activated, slope, gated = head_output(mixed, gate_pre, full_head_gain)
    attn_total = pair_sum(matmul_nt(gated, full_out))
    hidden_one = residual + attn_total
    inverse_two = inverse_rms(hidden_one)
    normed_two = (hidden_one * inverse_two * full_ffn_gain).astype(bf16)
    full_up_pair = ffn_all[:, : 2 * units]
    full_down = ffn_all[:, 2 * units :]
    ffn_both = matmul(normed_two, full_up_pair)
    ffn_pre, ffn_lin = ffn_both[:, :units], ffn_both[:, units:]
    ffn_silu, ffn_slope = silu_parts(ffn_pre)
    ffn_act = (ffn_silu * ffn_lin).astype(bf16)
    ffn_total = pair_sum(matmul_nt(ffn_act, full_down))
    output = (hidden_one + ffn_total).astype(bf16)

    act_grad = matmul(cotangent, full_down)
    down_grad = matmul_tn(cotangent, ffn_act).astype(bf16)
    pre_grad = (act_grad * ffn_lin * ffn_slope).astype(bf16)
    lin_grad = (act_grad * ffn_silu).astype(bf16)
    both_grad = jnp.concatenate([pre_grad, lin_grad], axis=1)
    up_pair_grad = matmul_tn(normed_two, both_grad).astype(bf16)
    normed_two_grad = pair_sum(matmul_nt(both_grad, full_up_pair))
    ffn_gain_grad = jnp.sum(normed_two_grad * hidden_one * inverse_two, axis=0)
    hidden_grad = cotangent.astype(f32) + norm_back(
        hidden_one, inverse_two, full_ffn_gain, normed_two_grad
    )
    hidden_low = hidden_grad.astype(bf16)
    out_grad = matmul_tn(hidden_low, gated).astype(bf16)
    ffn_part, hidden_after = lax.optimization_barrier(
        (jnp.concatenate([up_pair_grad, down_grad, out_grad], axis=1), hidden_low)
    )
    ffn_sums = lax.psum_scatter(ffn_part, "dp", scatter_dimension=0, tiled=True)
    gated_grad = matmul(hidden_after, full_out).reshape(mixed.shape)
    head_gain_part = pair_sum(jnp.sum(gated_grad * head_hat * activated, axis=(0, 1)))
    gate_pre_grad = (
        (gated_grad * head_hat * full_head_gain * slope).reshape(local, -1).astype(bf16)
    )
    mixed_grad = norm_back(mixed, inverse_head, full_head_gain * activated, gated_grad)
    rising = jnp.exp(cumul) * (segment_ids == seg_before).astype(f32)[:, None, None]
    local_back = jnp.einsum("thd,thv->hdv", query_f * rising, mixed_grad, precision=highest)
    back_in = entering(keeps_after, local_back, "dp", True, bf16)
    carried, found = mixer_backward(
        back_in,
        jnp.zeros_like(total),
        starts,
        seg_before,
        query_f,
        key_f,
        value_f,
        decays,
        segment_ids,
        mixed_grad,
        block,
    )
    query_vec, key_vec, value_vec, decay_local = found
    joined_after = []
    for hop in range(1, hops):
        at = jnp.minimum(place + hop, count - 1)
        same = lax.dynamic_index_in_dim(last_ids, at, 0, False) == lax.dynamic_index_in_dim(
            last_ids, at - 1, 0, False
        )
        joined_after.append((same & (place + hop < count)).astype(f32))
    decay_in = entering(joined_after, carried[1], "dp", True)
    decay_grad = decay_local + last_mask[:, None, None] * decay_in[None]
    rise_back = decay_grad * jax.nn.sigmoid(-rise_pre) / gate_scale
    bias_grad = jnp.sum(rise_back, axis=0)
    rise_grad = jnp.einsum("nr,nhd->hrd", low_rank, rise_back, precision=highest)
    proj_back = jnp.concatenate(
        [
            query_vec.reshape(local, -1).astype(bf16),
            key_vec.reshape(local, -1).astype(bf16),
            value_vec.reshape(local, -1).astype(bf16),
            gate_pre_grad,
        ],
        axis=1,
    )
    proj_grad = matmul_tn(normed_one, proj_back).astype(bf16)
    low_back = pair_sum(
        jnp.einsum("nhd,hrd->nr", rise_back, full_rise, precision=highest)
    ).astype(bf16)
    normed_one_grad = pair_sum(matmul_nt(proj_back, full_proj)) + matmul_nt(low_back, full_low)
    low_grad = matmul_tn(normed_one, low_back).astype(bf16)
    attn_gain_grad = jnp.sum(normed_one_grad * residual * inverse_one, axis=0)
    tokens_grad = hidden_grad + norm_back(residual, inverse_one, full_attn_gain, normed_one_grad)
    tiny_grad = jnp.concatenate(
        [
            rise_grad.reshape(heads, rank, count, dk_own).transpose(2, 0, 1, 3).reshape(count, -1),
            bias_grad.reshape(heads, count, dk_own).transpose(1, 0, 2).reshape(count, -1),
            head_gain_part.reshape(count, dv_own),
        ],
        axis=1,
    )
    tiny_grad = jnp.pad(tiny_grad, ((0, 0), (0, tiny_columns * rows - tiny_size + 1)))
    attn_part = jnp.concatenate(
        [
            proj_grad,
            low_grad,
            attn_gain_grad[:, None].astype(bf16),
            ffn_gain_grad[:, None].astype(bf16),
            tiny_grad.reshape(count * rows, tiny_columns).astype(bf16),
            jnp.zeros((count * rows, extra_width - used), bf16),
        ],
        axis=1,
    )
    attn_part, ffn_sums = lax.optimization_barrier((attn_part, ffn_sums))
    attn_sums = lax.psum_scatter(attn_part, "dp", scatter_dimension=0, tiled=True).astype(f32)
    ffn_sums = ffn_sums.astype(f32)
    tiny_sums = attn_sums[:, width + rank + 2 : width + used].reshape(-1)
    return (
        output,
        tokens_grad,
        attn_sums[:, width + rank],
        attn_sums[:, : ends[0]],
        attn_sums[:, ends[0] : ends[1]],
        attn_sums[:, ends[1] : ends[2]],
        attn_sums[:, ends[2] : ends[3]],
        attn_sums[:, width : width + rank],
        tiny_sums[:rise_size].reshape(heads, rank, dk_own),
        tiny_sums[rise_size : rise_size + bias_size].reshape(heads, dk_own),
        tiny_sums[start : start + dv_own],
        ffn_sums[:, 3 * units :],
        attn_sums[:, width + rank + 1],
        ffn_sums[:, :units],
        ffn_sums[:, units : 2 * units],
        ffn_sums[:, 2 * units : 3 * units],
    )


def solution(mesh):
    return jax.shard_map(
        body,
        mesh=mesh,
        in_specs=(
            P("dp", None),
            P("dp"),
            P("dp"),
            P("dp", "tensor"),
            P("dp", "tensor"),
            P("dp", "tensor"),
            P("dp", "tensor"),
            P("dp", None),
            P("tensor", None, "dp"),
            P("tensor", "dp"),
            P("dp"),
            P("dp", "tensor"),
            P("dp"),
            P("dp", "tensor"),
            P("dp", "tensor"),
            P("dp", "tensor"),
            P("dp", None),
        ),
        out_specs=(
            P("dp", None),
            P("dp", None),
            P("dp"),
            P("dp", "tensor"),
            P("dp", "tensor"),
            P("dp", "tensor"),
            P("dp", "tensor"),
            P("dp", None),
            P("tensor", None, "dp"),
            P("tensor", "dp"),
            P("dp"),
            P("dp", "tensor"),
            P("dp"),
            P("dp", "tensor"),
            P("dp", "tensor"),
            P("dp", "tensor"),
        ),
        check_vma=False,
    )
```
